128 devices in a mesh: prow: 8 (over x, y_lo), pcol: 16 (over y_hi, z, core).
Axes of the slice: x: 4, y: 4 (y_hi: 2, y_lo: 2; y = y_hi * 2 + y_lo), z: 4, core: 2. Of those that a mesh axis runs over, the one named last changes fastest.
Arguments:
- inverse_top: bfloat16 [128, 128, 128, 128], P('prow', 'pcol'), may hold values from -6 to 6
- rows_one: int32 [16, 64], replicated, may hold values from 0 to 127, as said below
- panel_one: bfloat16 [16, 64, 128, 128], P('pcol', 'prow'), may hold values from -0.0625 to 0.0625
- base_one: float32 [16, 128, 128], P('pcol'), may hold values from -6 to 6
- parent_two: int32 [16], replicated, may hold values from 0 to 15
- order_two: int32 [16, 64], replicated, may hold values from 0 to 63, as said below
- panel_two: bfloat16 [16, 64, 128, 128], P('pcol', 'prow'), may hold values from -0.0625 to 0.0625
- link_two: bfloat16 [16, 128, 128], P('pcol'), may hold values from -0.5 to 0.5
- base_two: float32 [16, 128, 128], P('pcol'), may hold values from -6 to 6
Outputs:
- column_one: bfloat16 [16, 64, 128, 128], P('pcol', 'prow')
- diagonal_one: bfloat16 [16, 128, 128], P('pcol')
- column_two: bfloat16 [16, 64, 128, 128], P('pcol', 'prow')
- upper_two: bfloat16 [16, 128, 128], P('pcol')
- diagonal_two: bfloat16 [16, 128, 128], P('pcol')
The draws below stay inside these ranges and needn't reach their ends.
Inputs may be any that keep to these rules, and one draw needn't show every extreme that they name: For every supernode k and process row p, rows_one[k, p * 8] to rows_one[k, p * 8 + 7] are 8 distinct ancestors between p * 16 and p * 16 + 15. In every draw some process column c holds 8 ancestors (ancestor // 8 == c) of every level-one supernode. Each block order_two[k, p * 8] to order_two[k, p * 8 + 7] is a permutation of p * 8 to p * 8 + 7.
All inputs are finite; a program needn't handle non-finite values.
Results may differ from the reference program's by a relative error of at most 0.024.
Values may be sent and summed in bfloat16 or wider, within the bound.
A program may use at most 192 MiB of HBM per device.

```python
import math
from functools import partial
import jax
import jax.numpy as jnp
import numpy as np
from jax import lax

TILE = 128
AP = 16
MP = 8
PCOLS = 16
NA = 128
AQ = 8
M = 64
NS1 = 16
NS2 = 16


def draw_rows_one(key, part):
    groups = M // MP
    split_keys = jax.random.split(jax.random.fold_in(key, 11), NS1 * groups)
    shuffled = jax.vmap(partial(jax.random.permutation, x=AP))(split_keys)
    picked = shuffled[:, :MP].reshape(NS1, groups, MP)
    full_keys = jax.random.split(jax.random.fold_in(key, 12), NS1)
    filled = jax.vmap(partial(jax.random.permutation, x=AQ))(full_keys)[:, :MP]
    chosen = jax.random.randint(jax.random.fold_in(key, 13), (2,), 0, 1 << 20)
    full_row = chosen[0] % groups
    full_class = chosen[1] % (AP // AQ)
    offsets = (jnp.arange(groups, dtype=jnp.int32) * AP)[None, :, None]
    drawn = offsets + picked
    special = (full_row * AP + full_class * AQ + filled)[:, None, :]
    is_full = (jnp.arange(groups, dtype=jnp.int32) == full_row)[None, :, None]
    return jnp.where(is_full, special, drawn).reshape(NS1, M).astype(jnp.int32)


def draw_order_two(key, part):
    groups = M // MP
    key_list = jax.random.split(jax.random.fold_in(key, 21), NS2 * groups)
    shuffled = jax.vmap(partial(jax.random.permutation, x=MP))(key_list).reshape(NS2, groups, MP)
    offsets = (jnp.arange(groups, dtype=jnp.int32) * MP)[None, :, None]
    return (shuffled + offsets).reshape(NS2, M).astype(jnp.int32)


def with_ends(array, stream_key, smallest, top_value):
    index_at = [jax.random.randint(jax.random.fold_in(stream_key, axis), (), 0, length) for axis, length in enumerate(array.shape)]
    longest = array.shape.index(max(array.shape))
    next_to = index_at[:longest] + [(index_at[longest] + 1) % array.shape[longest]] + index_at[longest + 1:]
    return array.at[tuple(index_at)].set(smallest).at[tuple(next_to)].set(top_value)


def block_levels(stream_key, dims, pieces, smallest, top_value):
    def one(dim, parts):
        heights = jax.random.uniform(jax.random.fold_in(jax.random.fold_in(stream_key, 6), dim), (parts,), jnp.float32, smallest / len(pieces), top_value / len(pieces))
        return jnp.repeat(jnp.exp(heights), dims[dim] // parts).reshape((-1,) + (1,) * (len(dims) - dim - 1))

    gain = one(*pieces[0])
    for cut in pieces[1:]:
        gain = gain * one(*cut)
    return gain


def rank_bounds(amount, slope):
    portions = [(1 << 20) // math.isqrt(rank ** slope) + 1 for rank in range(1, amount + 1)]
    scale = 1 + sum(portions) // (1 << 30)
    return np.cumsum(np.array([max(1, weight // scale) for weight in portions]))


def ranked_ids(key, shape, amount, skew):
    table = rank_bounds(amount, skew)
    ticket = jax.random.randint(jax.random.fold_in(key, 1), shape, 0, int(table[amount - 1]))
    standing = jnp.searchsorted(jnp.asarray(table, jnp.int32), ticket, side="right")
    return jax.random.permutation(jax.random.fold_in(key, 2), amount)[standing].astype(jnp.int32)


def scatter_about(own_key, dims, width, limit, cuts=(), held_as=jnp.bfloat16):
    loudness = block_levels(own_key, dims, cuts, -0.22, 0.18) if cuts else 1.0
    entries = jax.random.normal(own_key, dims, jnp.float32) * width * loudness
    return jnp.minimum(jnp.maximum(entries, -limit), limit).astype(held_as)


def setup_inputs(seed: int = 0) -> dict:
    streams_of = jax.random.split(jax.random.key(seed), 10)
    return {
        "inverse_top": scatter_about(streams_of[0], (NA, NA, TILE, TILE), 1.0, 6.0, ((0, 8), (1, 16))),
        "rows_one": draw_rows_one(jax.random.fold_in(streams_of[9], 71), 0),
        "panel_one": scatter_about(streams_of[2], (NS1, M, TILE, TILE), (M * TILE) ** -0.5, 0.0625, ((0, 16), (1, 8))),
        "base_one": scatter_about(streams_of[3], (NS1, TILE, TILE), 1.0, 6.0, ((0, 16),), jnp.float32),
        "parent_two": with_ends(ranked_ids(streams_of[4], (NS2,), NS1, 2), jax.random.fold_in(streams_of[4], 3), 0, NS1 - 1).astype(jnp.int32),
        "order_two": draw_order_two(jax.random.fold_in(streams_of[9], 71), 0),
        "panel_two": scatter_about(streams_of[6], (NS2, M, TILE, TILE), (M * TILE) ** -0.5, 0.0625, ((0, 16), (1, 8))),
        "link_two": scatter_about(streams_of[7], (NS2, TILE, TILE), TILE ** -0.5, 0.5, ((0, 16),)),
        "base_two": scatter_about(streams_of[8], (NS2, TILE, TILE), 1.0, 6.0, ((0, 16),), jnp.float32),
    }


def level_columns(inverse_top, ancestor_rows, panel_tiles):
    classes = jnp.arange(PCOLS, dtype=jnp.int32)

    def one_node(operands):
        ancestors, panels = operands
        submatrix = inverse_top[ancestors[:, None], ancestors[None, :]].astype(jnp.float32)
        products = jnp.einsum("mnij,njk->mnik", submatrix, panels.astype(jnp.float32))
        member = (ancestors[None, :] // AQ == classes[:, None]).astype(jnp.float32)
        partial_value = jnp.einsum("qn,mnik->qmik", member, products).astype(jnp.bfloat16)
        partial_value = lax.optimization_barrier(partial_value).astype(jnp.float32)
        return -jnp.sum(partial_value, axis=0)

    return lax.map(one_node, (ancestor_rows, panel_tiles))


def reference(inverse_top, rows_one, panel_one, base_one, parent_two, order_two, panel_two, link_two, base_two):
    column_one = level_columns(inverse_top, rows_one, panel_one).astype(jnp.bfloat16)
    diag_sum = jnp.einsum("kmij,kmil->kjl", panel_one.astype(jnp.float32), column_one.astype(jnp.float32))
    diagonal_one = (base_one - diag_sum).astype(jnp.bfloat16)
    rows_two = jnp.take_along_axis(rows_one[parent_two], order_two, axis=1)
    terms_two = level_columns(inverse_top, rows_two, panel_two)
    near_two = column_one[parent_two[:, None], order_two]
    carried = jnp.einsum("kmij,kjl->kmil", near_two.astype(jnp.float32), link_two.astype(jnp.float32))
    column_two = (terms_two - carried).astype(jnp.bfloat16)
    parent_term = jnp.einsum("kij,kjl->kil", diagonal_one[parent_two].astype(jnp.float32), link_two.astype(jnp.float32))
    upper_sum = jnp.einsum("kmij,kmil->kjl", near_two.astype(jnp.float32), panel_two.astype(jnp.float32))
    upper_two = (-(parent_term + upper_sum)).astype(jnp.bfloat16)
    link_term = jnp.einsum("kij,kil->kjl", link_two.astype(jnp.float32), upper_two.astype(jnp.float32))
    lower_sum = jnp.einsum("kmij,kmil->kjl", panel_two.astype(jnp.float32), column_two.astype(jnp.float32))
    diagonal_two = (base_two - link_term - lower_sum).astype(jnp.bfloat16)
    return (column_one, diagonal_one, column_two, upper_two, diagonal_two)
```

```python
import functools

import jax
import jax.numpy as jnp
from jax import lax
from jax.experimental import pallas as pl
from jax.experimental.pallas import tpu as pltpu
from jax.sharding import PartitionSpec as P

F32 = jnp.float32
BF = jnp.bfloat16
COL = 9


def tdot(a, b):
    return lax.dot_general(a, b, (((0,), (0,)), ((), ())), preferred_element_type=F32)


def kernel(
    rows_ref, parent_ref, order_ref, inv_ref, p1_ref, b1_ref, p2_ref, link_ref, b2_ref,
    c1_ref, d1_ref, c2_ref, u2_ref, d2_ref,
    tf, xb, yp, fb, nb, ys, yr, gz, sc, cc, yb, dd, ar, pv1, pv2, keep, snd, rcv, loc,
):
    tl = inv_ref.shape[-1]
    p = lax.axis_index("prow")
    c = lax.axis_index("pcol")
    x, yl = p // 2, p % 2
    yh, j, z, q = c // 8, c // 2, (c // 2) % 4, c % 2
    xl, xr, xo = (x + 3) % 4, (x + 1) % 4, (x + 2) % 4
    zl, zr, zo = (z + 3) % 4, (z + 1) % 4, (z + 2) % 4

    left_x = (2 * xl + yl, c)
    right_x = (2 * xr + yl, c)
    mate_y = (2 * x + 1 - yl, c)
    left_z = (p, 8 * yh + 2 * zl + q)
    right_z = (p, 8 * yh + 2 * zr + q)
    core = (p, 2 * j + 1 - q)
    far_y = (p, 8 * (1 - yh) + 2 * z + q)
    turned = (j, 2 * p + q)


    def remote(src, dst, at, to, send_at=None):
        return pltpu.make_async_remote_copy(
            src_ref=src, dst_ref=dst, send_sem=snd.at[at if send_at is None else send_at], recv_sem=rcv.at[at],
            device_id=to, device_id_type=pl.DeviceIdType.MESH)

    T_AT = 0
    X_AT = 1
    XS_AT = 17
    FAR_AT = 21
    NE_AT = 29
    NL_AT = 37
    Y_AT = 45
    G_AT = 47
    C_AT = 51
    D_AT = 52
    A_AT = 53
    panels = (p1_ref, p2_ref)

    slots = (p, 2 * x + 1 - yl, 2 * xl + yl, 2 * xr + yl, 2 * xl + 1 - yl, 2 * xr + 1 - yl, 2 * xo + yl, 2 * xo + 1 - yl)

    def turn(l):
        return remote(panels[l].at[0], xb.at[l, j], X_AT + 8 * l, turned)

    def turn_here(l):
        return pltpu.make_async_copy(panels[l].at[0], xb.at[l, p], loc.at[l])

    def send_y(l):
        return remote(xb.at[l, p], xb.at[l, p], X_AT + 8 * l + 1, mate_y)

    def send_x(l, which, to_right):
        s = slots[which]
        at = X_AT + 8 * l + 2 + 2 * which + (0 if to_right else 1)
        return remote(xb.at[l, s], xb.at[l, s], at, right_x if to_right else left_x)

    def forward(l, which, to_right):
        s = slots[2 + 2 * which + (0 if to_right else 1)]
        part = pl.ds(0, 4) if to_right else pl.ds(4, 4)
        at = X_AT + 8 * l + 6 + which
        sat = at if to_right else XS_AT + 2 * l + which
        return remote(xb.at[l, s, part], xb.at[l, s, part], at, right_x if to_right else left_x, sat)

    def arrived(l, i):
        s = slots[i]
        return remote(xb.at[l, s], xb.at[l, s], X_AT + 8 * l + i, right_x)

    def far(l, yd, dr):
        h = 4 * yd + zo
        part = pl.ds(4 * dr, 4)
        return remote(yp.at[l, h, part], fb.at[l, yd, dr], FAR_AT + 4 * l + 2 * yd + dr, (right_z, left_z)[dr])

    def near_early(l, yd, dr):
        h = 4 * yd + (zr, zl)[dr]
        part = pl.ds(4 - 4 * dr, 4)
        return remote(yp.at[l, h, part], nb.at[l, yd, dr, part], NE_AT + 4 * l + 2 * yd + dr, (right_z, left_z)[dr])

    def near_late(l, yd, dr):
        h = 4 * yd + (zr, zl)[dr]
        part = pl.ds(4 * dr, 4)
        return remote(yp.at[l, h, part], nb.at[l, yd, dr, part], NL_AT + 4 * l + 2 * yd + dr, (right_z, left_z)[dr])

    def across(l):
        return remote(ys.at[l], yr.at[l], Y_AT + l, far_y)

    t_here = pltpu.make_async_copy(inv_ref, tf.at[q], loc.at[2])
    t_here.start()
    v1 = pltpu.make_async_copy(p1_ref.at[0], pv1, loc.at[3])
    v2 = pltpu.make_async_copy(p2_ref.at[0], pv2, loc.at[4])
    v1.start()
    v2.start()

    barrier = pltpu.get_barrier_semaphore()

    def greet(to):
        pl.semaphore_signal(barrier, inc=1, device_id=to, device_id_type=pl.DeviceIdType.MESH)

    for d in range(1, 8):
        greet(((p + d) % 8, c))
    for to in (left_z, right_z, core, far_y):
        greet(to)

    @pl.when(p != j)
    def _():
        greet(turned)
        pl.semaphore_wait(barrier, 12)

    @pl.when(p == j)
    def _():
        pl.semaphore_wait(barrier, 11)

    def start_turn(l):
        @pl.when(p != j)
        def _():
            turn(l).start()

        @pl.when(p == j)
        def _():
            turn_here(l).start()

    def wait_turn(l):
        @pl.when(p != j)
        def _():
            arrived(l, 0).wait_recv()

        @pl.when(p == j)
        def _():
            turn_here(l).wait()

    sent = []

    def go(copy):
        copy.start()
        sent.append(copy)

    def own_out(l):
        go(send_y(l))
        go(send_x(l, 0, True))
        go(send_x(l, 0, False))

    def mate_out(l):
        arrived(l, 1).wait_recv()
        go(send_x(l, 1, True))
        go(send_x(l, 1, False))

    def relay(l, which):
        arrived(l, 2 + 2 * which).wait_recv()
        go(forward(l, which, True))
        arrived(l, 3 + 2 * which).wait_recv()
        go(forward(l, which, False))

    def row_at(l, k, i):
        if l == 0:
            return rows_ref[k, i]
        return rows_ref[parent_ref[k], order_ref[k, i]]

    def products(l, i):
        h = slots[i]
        k = 2 * h + q
        cols = [row_at(l, k, 8 * j + n) for n in range(8)]
        cols = [((a >> 3) & 1, a & 7) for a in cols]

        def one(m, carry):
            r = row_at(l, k, 8 * p + m) & 15
            wide = jnp.concatenate([tf[a, r, b] for a, b in cols], axis=1)
            tall = xb[l, h].reshape(8 * tl, tl)
            yp[l, h, m] = jnp.dot(wide, tall, preferred_element_type=F32).astype(BF)
            return carry

        lax.fori_loop(0, 8, one, 0)
        yd, d = h // 4, (h % 4 + 4 - z) % 4

        @pl.when(d == 2)
        def _():
            far(l, yd, 0).start()
            far(l, yd, 1).start()

        @pl.when(d == 1)
        def _():
            near_early(l, yd, 0).start()

        @pl.when(d == 3)
        def _():
            near_early(l, yd, 1).start()

    def pass_on(l):
        for yd in range(2):
            for dr in range(2):
                far(l, yd, dr).wait_recv()
                h = 4 * yd + (zr, zl)[dr]
                part = pl.ds(4 * dr, 4)
                yp[l, h, part] = (yp[l, h, part].astype(F32) + fb[l, yd, dr].astype(F32)).astype(BF)
                go(near_late(l, yd, dr))

    def meet(l):
        for yd in range(2):
            for dr in range(2):
                near_early(l, yd, dr).wait_recv()
                near_late(l, yd, dr).wait_recv()

        def total(yd, m):
            h = 4 * yd + z
            return yp[l, h, m].astype(F32) + nb[l, yd, 0, m].astype(F32) + nb[l, yd, 1, m].astype(F32)

        for m in range(8):
            ys[l, m] = total(1 - yh, m).astype(BF)
        go(across(l))
        for m in range(8):
            keep[l, m] = total(yh, m)

    def spread(t):
        copies = [
            remote(ar.at[t, p], ar.at[t, p], A_AT + t, ((p + d) % 8, c)) for d in range(1, 8)
        ]
        for copy in copies:
            copy.start()

    def spread_all(t):
        return remote(ar.at[t, pl.ds(0, 7)], ar.at[t, pl.ds(0, 7)], A_AT + t, right_x)

    def spread_sum(t):
        spread_all(t).wait_recv()
        total = ar[t, 0].astype(F32)
        for i in range(1, 8):
            total = total + ar[t, i].astype(F32)
        return total

    start_turn(0)
    t_there = remote(inv_ref, tf.at[q], T_AT, core)
    t_there.start()
    sent.append(t_there)
    wait_turn(0)
    own_out(0)
    start_turn(1)
    mate_out(0)
    t_here.wait()
    t_there.wait_recv()
    products(0, 0)
    products(0, 1)
    relay(0, 0)
    products(0, 2)
    products(0, 3)
    relay(0, 1)
    wait_turn(1)
    own_out(1)
    products(0, 4)
    products(0, 5)
    mate_out(1)
    arrived(0, 6).wait_recv()
    products(0, 6)
    arrived(0, 7).wait_recv()
    products(0, 7)
    pass_on(0)
    products(1, 0)
    products(1, 1)
    relay(1, 0)
    products(1, 2)
    products(1, 3)
    meet(0)
    relay(1, 1)
    products(1, 4)
    products(1, 5)
    v1.wait()
    v2.wait()

    across(0).wait_recv()
    for m in range(8):
        tile = (-(keep[0, m] + yr[0, m].astype(F32))).astype(BF)
        c1_ref[0, m] = tile
        gz[z, m] = tile
    share = tdot(pv1[...].reshape(8 * tl, tl), c1_ref[0].reshape(8 * tl, tl))
    ar[0, p] = share.astype(BF)
    spread(0)
    first = jnp.where(p == 0, 1.0, 0.0).astype(F32)
    gz[z, 8] = (b1_ref[0] * first - share).astype(BF)
    g_right = remote(gz.at[z], gz.at[z], G_AT, right_z)
    g_left = remote(gz.at[z], gz.at[z], G_AT + 1, left_z)
    go(g_right)
    go(g_left)

    arrived(1, 6).wait_recv()
    products(1, 6)
    arrived(1, 7).wait_recv()
    products(1, 7)
    pass_on(1)

    remote(gz.at[zl], gz.at[zl], G_AT, right_z).wait_recv()
    go(remote(gz.at[zl, pl.ds(0, 5)], gz.at[zl, pl.ds(0, 5)], G_AT + 2, right_z))
    remote(gz.at[zr], gz.at[zr], G_AT + 1, right_z).wait_recv()
    go(remote(gz.at[zr, pl.ds(5, 4)], gz.at[zr, pl.ds(5, 4)], G_AT + 2, left_z, G_AT + 3))

    d1_ref[0] = (b1_ref[0] - spread_sum(0)).astype(BF)

    remote(gz.at[zo], gz.at[zo], G_AT + 2, right_z).wait_recv()
    for yd in range(2):
        there = parent_ref[8 * yd + 2 * z + 1 - q]
        sc[yd] = gz[(there >> 1) & 3]
    to_core = remote(sc, cc.at[q], C_AT, core)
    go(to_core)
    for yd in range(2):
        here = parent_ref[8 * yd + 2 * z + q]
        cc[q, yd] = gz[(here >> 1) & 3]
    meet(1)
    to_core.wait_recv()
    yb[...] = cc[parent_ref[8 * (1 - yh) + 2 * z + q] & 1, 1 - yh]
    to_far = remote(yb, dd.at[yh], D_AT, far_y)
    go(to_far)
    mine = parent_ref[c]
    dd[yh] = cc[mine & 1, yh]
    to_far.wait_recv()

    link = link_ref[0]
    around = (mine >> 3) & 1
    near = [dd[around, order_ref[c, 8 * p + m] & 7] for m in range(8)]
    near_all = jnp.concatenate(near, axis=0)
    upper = tdot(near_all, pv2[...].reshape(8 * tl, tl)) + jnp.dot(dd[around, 8], link, preferred_element_type=F32)
    ar[1, p] = upper.astype(BF)
    spread(1)
    for m in range(8):
        keep[1, m] = keep[1, m] + jnp.dot(near[m], link, preferred_element_type=F32)
    across(1).wait_recv()
    for m in range(8):
        c2_ref[0, m] = (-(keep[1, m] + yr[1, m].astype(F32))).astype(BF)
    lower = tdot(pv2[...].reshape(8 * tl, tl), c2_ref[0].reshape(8 * tl, tl))
    ar[2, p] = lower.astype(BF)
    spread(2)
    u2 = (-spread_sum(1)).astype(BF)
    u2_ref[0] = u2
    rest = b2_ref[0] - tdot(link, u2)
    d2_ref[0] = (rest - spread_sum(2)).astype(BF)

    for copy in sent:
        copy.wait_send()
    for l in range(2):
        @pl.when(p != j)
        def _():
            turn(l).wait_send()

        for yd in range(2):
            for dr in range(2):
                far(l, yd, dr).wait_send()
                near_early(l, yd, dr).wait_send()
    for t in range(3):
        spread_all(t).wait_send()


def local(inverse_top, rows_one, panel_one, base_one, parent_two, order_two, panel_two, link_two, base_two):
    tl = inverse_top.shape[-1]
    vm = lambda *s: pltpu.VMEM(s + (tl, tl), BF)
    anyw = pl.BlockSpec(memory_space=pl.ANY)
    smem = pl.BlockSpec(memory_space=pltpu.SMEM)
    vmem = pl.BlockSpec(memory_space=pltpu.VMEM)
    one = jax.ShapeDtypeStruct(panel_one.shape, BF)
    tile = jax.ShapeDtypeStruct(link_two.shape, BF)
    return pl.pallas_call(
        kernel,
        out_shape=(one, tile, one, tile, tile),
        in_specs=[smem, smem, smem, anyw, anyw, vmem, anyw, vmem, vmem],
        out_specs=[vmem] * 5,
        scratch_shapes=[
            vm(2, 16, 8), vm(2, 8, 8), vm(2, 8, 8),
            vm(2, 2, 2, 4), vm(2, 2, 2, 8), vm(2, 8), vm(2, 8),
            vm(4, COL), vm(2, COL), vm(2, 2, COL), vm(COL), vm(2, COL), vm(3, 8),
            vm(8), vm(8), pltpu.VMEM((2, 8, tl, tl), F32),
            pltpu.SemaphoreType.DMA((56,)), pltpu.SemaphoreType.DMA((56,)), pltpu.SemaphoreType.DMA((5,)),
        ],
        compiler_params=pltpu.CompilerParams(
            collective_id=0, has_side_effects=True, vmem_limit_bytes=56 * 1024 * 1024),
    )(rows_one, parent_two, order_two, inverse_top, panel_one, base_one, panel_two, link_two, base_two)


def solution(mesh):
    return jax.shard_map(
        local,
        mesh=mesh,
        in_specs=(
            P("prow", "pcol", None, None), P(), P("pcol", "prow", None, None), P("pcol", None, None), P(),
            P(), P("pcol", "prow", None, None), P("pcol", None, None), P("pcol", None, None),
        ),
        out_specs=(
            P("pcol", "prow", None, None), P("pcol", None, None), P("pcol", "prow", None, None),
            P("pcol", None, None), P("pcol", None, None),
        ),
        check_vma=False,
    )
```

```python
import functools

import jax
import jax.numpy as jnp
from jax import lax
from jax.experimental import pallas as pl
from jax.experimental.pallas import tpu as pltpu
from jax.sharding import PartitionSpec as P

F32 = jnp.float32
BF = jnp.bfloat16
COL = 9


def tdot(a, b):
    return lax.dot_general(a, b, (((0,), (0,)), ((), ())), preferred_element_type=F32)


def kernel(
    rows_ref, parent_ref, order_ref, inv_ref, p1_ref, b1_ref, p2_ref, link_ref, b2_ref,
    out_ref,
    tf, xb, yp, fb, nb, ys, yr, gz, sc, cc, yb, dd, ar, pv1, pv2, keep, snd, rcv, loc,
):
    tl = inv_ref.shape[-1]
    p = lax.axis_index("prow")
    c = lax.axis_index("pcol")
    x, yl = p // 2, p % 2
    yh, j, z, q = c // 8, c // 2, (c // 2) % 4, c % 2
    xl, xr, xo = (x + 3) % 4, (x + 1) % 4, (x + 2) % 4
    zl, zr, zo = (z + 3) % 4, (z + 1) % 4, (z + 2) % 4

    left_x = (2 * xl + yl, c)
    right_x = (2 * xr + yl, c)
    mate_y = (2 * x + 1 - yl, c)
    left_z = (p, 8 * yh + 2 * zl + q)
    right_z = (p, 8 * yh + 2 * zr + q)
    core = (p, 2 * j + 1 - q)
    far_y = (p, 8 * (1 - yh) + 2 * z + q)

    def held(slot):
        return 4 * (slot % 2) + (slot // 2 + z) % 4

    to_p = 2 * ((z + 4 - p % 4) % 4) + yh
    turned = (to_p, 2 * p + q)
    source = (j, 2 * held(p) + q)
    stays = jnp.logical_and(to_p == p, c == 2 * p + q)

    parity = (yl, 1 - yl, 1 - yh, yh)
    level = (0, 0, 1, 1)

    def slot(t, xs):
        return 2 * xs + parity[t]

    def remote(src, dst, at, to, send_at=None):
        return pltpu.make_async_remote_copy(
            src_ref=src, dst_ref=dst, send_sem=snd.at[at if send_at is None else send_at], recv_sem=rcv.at[at],
            device_id=to, device_id_type=pl.DeviceIdType.MESH)

    T_AT, TURN_AT, MATE_AT, BASE_AT, FWD_AT, FWD_LEFT_AT = 0, 1, 3, 5, 13, 17
    FAR_AT, NE_AT, NL_AT, Y_AT, G_AT, C_AT, D_AT, A_AT = 21, 29, 37, 45, 47, 51, 52, 53
    panels = (p1_ref, p2_ref)

    def turn(l):
        return remote(panels[l].at[0], xb.at[l, to_p], TURN_AT + l, turned)

    def turn_here(l):
        return pltpu.make_async_copy(panels[l].at[0], xb.at[l, p], loc.at[l])

    def mate(l):
        return remote(xb.at[l, p], xb.at[l, p], MATE_AT + l, mate_y)

    def base(t, dr):
        at = xb.at[level[t], slot(t, x)]
        return remote(at, at, BASE_AT + 2 * t + dr, (right_x, left_x)[dr])

    def base_in(t, dr):
        at = xb.at[level[t], slot(t, (xl, xr)[dr])]
        return remote(at, at, BASE_AT + 2 * t + dr, right_x)

    def forward(t, dr):
        at = xb.at[level[t], slot(t, (xl, xr)[dr]), pl.ds(4 * dr, 4)]
        return remote(at, at, FWD_AT + t, (right_x, left_x)[dr], (FWD_AT, FWD_LEFT_AT)[dr] + t)

    def forward_in(t):
        at = xb.at[level[t], slot(t, xo)]
        return remote(at, at, FWD_AT + t, right_x)

    def far(t, dr):
        return remote(yp.at[t, zo, pl.ds(4 * dr, 4)], fb.at[t, dr], FAR_AT + 2 * t + dr, (right_z, left_z)[dr])

    def near_early(t, dr):
        part = pl.ds(4 - 4 * dr, 4)
        return remote(yp.at[t, (zr, zl)[dr], part], nb.at[t, dr, part], NE_AT + 2 * t + dr, (right_z, left_z)[dr])

    def near_late(t, dr):
        part = pl.ds(4 * dr, 4)
        return remote(yp.at[t, (zr, zl)[dr], part], nb.at[t, dr, part], NL_AT + 2 * t + dr, (right_z, left_z)[dr])

    def across(l):
        return remote(ys.at[l], yr.at[l], Y_AT + l, far_y)

    t_here = pltpu.make_async_copy(inv_ref, tf.at[q], loc.at[2])
    t_here.start()
    v1 = pltpu.make_async_copy(p1_ref.at[0], pv1, loc.at[3])
    v2 = pltpu.make_async_copy(p2_ref.at[0], pv2, loc.at[4])
    v1.start()
    v2.start()

    barrier = pltpu.get_barrier_semaphore()

    def greet(to):
        pl.semaphore_signal(barrier, inc=1, device_id=to, device_id_type=pl.DeviceIdType.MESH)

    @pl.when(jnp.logical_not(stays))
    def _():
        greet(source)

    for d in range(1, 8):
        greet(((p + d) % 8, c))
    for to in (left_z, right_z, core, far_y):
        greet(to)

    @pl.when(jnp.logical_not(stays))
    def _():
        pl.semaphore_wait(barrier, 12)

    @pl.when(stays)
    def _():
        pl.semaphore_wait(barrier, 11)

    def start_turn(l):
        @pl.when(jnp.logical_not(stays))
        def _():
            turn(l).start()

        @pl.when(stays)
        def _():
            turn_here(l).start()

    def wait_turn(l):
        @pl.when(jnp.logical_not(stays))
        def _():
            remote(xb.at[l, p], xb.at[l, p], TURN_AT + l, right_x).wait_recv()

        @pl.when(stays)
        def _():
            turn_here(l).wait()

    sent = []

    def go(copy):
        copy.start()
        sent.append(copy)

    def wait_mate(l):
        s = 2 * x + 1 - yl
        remote(xb.at[l, s], xb.at[l, s], MATE_AT + l, right_x).wait_recv()

    def base_out(t):
        go(base(t, 0))
        go(base(t, 1))

    def relay(t):
        for dr in range(2):
            base_in(t, dr).wait_recv()
            go(forward(t, dr))

    def row_at(l, k, i):
        if l == 0:
            return rows_ref[k, i]
        return rows_ref[parent_ref[k], order_ref[k, i]]

    def products(t, xs):
        l, s, zh = level[t], slot(t, xs), (xs + z) % 4
        k = 2 * held(s) + q
        cols = [row_at(l, k, 8 * j + n) for n in range(8)]
        cols = [((a >> 3) & 1, a & 7) for a in cols]

        def one(m, carry):
            r = row_at(l, k, 8 * p + m) & 15
            wide = jnp.concatenate([tf[a, r, b] for a, b in cols], axis=1)
            tall = xb[l, s].reshape(8 * tl, tl)
            yp[t, zh, m] = jnp.dot(wide, tall, preferred_element_type=F32).astype(BF)
            return carry

        lax.fori_loop(0, 8, one, 0)

        @pl.when(xs == 2)
        def _():
            far(t, 0).start()
            far(t, 1).start()

        @pl.when(xs == 1)
        def _():
            near_early(t, 0).start()

        @pl.when(xs == 3)
        def _():
            near_early(t, 1).start()

    def pass_on(t):
        for dr in range(2):
            far(t, dr).wait_recv()
            zh, part = (zr, zl)[dr], pl.ds(4 * dr, 4)
            yp[t, zh, part] = (yp[t, zh, part].astype(F32) + fb[t, dr].astype(F32)).astype(BF)
            go(near_late(t, dr))

    def meet(t):
        l = level[t]
        for dr in range(2):
            near_early(t, dr).wait_recv()
            near_late(t, dr).wait_recv()

        def total(m):
            return yp[t, z, m].astype(F32) + nb[t, 0, m].astype(F32) + nb[t, 1, m].astype(F32)

        def cross():
            for m in range(8):
                ys[l, m] = total(m).astype(BF)
            across(l).start()

        def stay():
            for m in range(8):
                keep[l, m] = total(m)

        if t == 2:
            cross()
        elif t == 3:
            stay()
        else:
            pl.when(parity[t] != yh)(cross)
            pl.when(parity[t] == yh)(stay)

    def spread(t):
        for d in range(1, 8):
            remote(ar.at[t, p], ar.at[t, p], A_AT + t, ((p + d) % 8, c)).start()

    def spread_all(t):
        return remote(ar.at[t, pl.ds(0, 7)], ar.at[t, pl.ds(0, 7)], A_AT + t, right_x)

    def spread_sum(t):
        spread_all(t).wait_recv()
        total = ar[t, 0].astype(F32)
        for i in range(1, 8):
            total = total + ar[t, i].astype(F32)
        return total

    start_turn(0)
    t_there = remote(inv_ref, tf.at[q], T_AT, core)
    go(t_there)
    wait_turn(0)
    go(mate(0))
    base_out(0)
    start_turn(1)
    t_here.wait()
    t_there.wait_recv()
    products(0, x)
    wait_mate(0)
    base_out(1)
    relay(0)
    products(1, x)
    products(0, xl)
    products(0, xr)
    wait_turn(1)
    go(mate(1))
    forward_in(0).wait_recv()
    products(0, xo)
    wait_mate(1)
    base_out(2)
    relay(1)
    products(1, xl)
    products(1, xr)
    pass_on(0)
    base_out(3)
    forward_in(1).wait_recv()
    products(1, xo)
    relay(2)
    products(2, x)
    meet(0)
    pass_on(1)
    products(3, x)
    products(2, xl)
    products(2, xr)
    meet(1)
    relay(3)
    forward_in(2).wait_recv()
    products(2, xo)
    v1.wait()
    v2.wait()

    across(0).wait_recv()
    for m in range(8):
        tile = (-(keep[0, m] + yr[0, m].astype(F32))).astype(BF)
        out_ref[m] = tile
        gz[z, m] = tile
    share = tdot(pv1[...].reshape(8 * tl, tl), gz[z, pl.ds(0, 8)].reshape(8 * tl, tl))
    ar[0, p] = share.astype(BF)
    first = jnp.where(p == 0, 1.0, 0.0).astype(F32)
    gz[z, 8] = (b1_ref[0] * first - share).astype(BF)
    g_right = remote(gz.at[z], gz.at[z], G_AT, right_z)
    g_left = remote(gz.at[z], gz.at[z], G_AT + 1, left_z)
    go(g_right)
    go(g_left)
    spread(0)

    pass_on(2)
    products(3, xl)
    products(3, xr)
    forward_in(3).wait_recv()
    products(3, xo)
    pass_on(3)
    meet(2)

    remote(gz.at[zl], gz.at[zl], G_AT, right_z).wait_recv()
    go(remote(gz.at[zl, pl.ds(0, 5)], gz.at[zl, pl.ds(0, 5)], G_AT + 2, right_z))
    remote(gz.at[zr], gz.at[zr], G_AT + 1, right_z).wait_recv()
    go(remote(gz.at[zr, pl.ds(5, 4)], gz.at[zr, pl.ds(5, 4)], G_AT + 2, left_z, G_AT + 3))

    out_ref[16] = (b1_ref[0] - spread_sum(0)).astype(BF)

    remote(gz.at[zo], gz.at[zo], G_AT + 2, right_z).wait_recv()
    for yd in range(2):
        there = parent_ref[8 * yd + 2 * z + 1 - q]
        sc[yd] = gz[(there >> 1) & 3]
    to_core = remote(sc, cc.at[q], C_AT, core)
    go(to_core)
    for yd in range(2):
        here = parent_ref[8 * yd + 2 * z + q]
        cc[q, yd] = gz[(here >> 1) & 3]
    to_core.wait_recv()
    yb[...] = cc[parent_ref[8 * (1 - yh) + 2 * z + q] & 1, 1 - yh]
    to_far = remote(yb, dd.at[yh], D_AT, far_y)
    go(to_far)
    mine = parent_ref[c]
    dd[yh] = cc[mine & 1, yh]
    meet(3)
    to_far.wait_recv()

    link = link_ref[0]
    around = (mine >> 3) & 1
    near = [dd[around, order_ref[c, 8 * p + m] & 7] for m in range(8)]
    near_all = jnp.concatenate(near, axis=0)
    upper = tdot(near_all, pv2[...].reshape(8 * tl, tl)) + jnp.dot(dd[around, 8], link, preferred_element_type=F32)
    ar[1, p] = upper.astype(BF)
    spread(1)
    for m in range(8):
        keep[1, m] = keep[1, m] + jnp.dot(near[m], link, preferred_element_type=F32)
    across(1).wait_recv()
    for m in range(8):
        out_ref[8 + m] = (-(keep[1, m] + yr[1, m].astype(F32))).astype(BF)
    lower = tdot(pv2[...].reshape(8 * tl, tl), out_ref[pl.ds(8, 8)].reshape(8 * tl, tl))
    ar[2, p] = lower.astype(BF)
    spread(2)
    u2 = (-spread_sum(1)).astype(BF)
    out_ref[17] = u2
    rest = b2_ref[0] - tdot(link, u2)
    out_ref[18] = (rest - spread_sum(2)).astype(BF)

    for copy in sent:
        copy.wait_send()
    for l in range(2):
        @pl.when(jnp.logical_not(stays))
        def _():
            turn(l).wait_send()

        across(l).wait_send()
    for t in range(4):
        for dr in range(2):
            far(t, dr).wait_send()
            near_early(t, dr).wait_send()
    for t in range(3):
        spread_all(t).wait_send()


def unpack(all_ref, c1_ref, d1_ref, c2_ref, u2_ref, d2_ref):
    c1_ref[0] = all_ref[pl.ds(0, 8)]
    c2_ref[0] = all_ref[pl.ds(8, 8)]
    d1_ref[0] = all_ref[16]
    u2_ref[0] = all_ref[17]
    d2_ref[0] = all_ref[18]


def local(inverse_top, rows_one, panel_one, base_one, parent_two, order_two, panel_two, link_two, base_two):
    tl = inverse_top.shape[-1]
    vm = lambda *s: pltpu.VMEM(s + (tl, tl), BF)
    anyw = pl.BlockSpec(memory_space=pl.ANY)
    smem = pl.BlockSpec(memory_space=pltpu.SMEM)
    vmem = pl.BlockSpec(memory_space=pltpu.VMEM)
    one = jax.ShapeDtypeStruct(panel_one.shape, BF)
    tile = jax.ShapeDtypeStruct(link_two.shape, BF)
    packed = pl.pallas_call(
        kernel,
        out_shape=jax.ShapeDtypeStruct((19, tl, tl), BF),
        in_specs=[smem, smem, smem, anyw, anyw, vmem, anyw, vmem, vmem],
        out_specs=vmem,
        scratch_shapes=[
            vm(2, 16, 8), vm(2, 8, 8), vm(4, 4, 8),
            vm(4, 2, 4), vm(4, 2, 8), vm(2, 8), vm(2, 8),
            vm(4, COL), vm(2, COL), vm(2, 2, COL), vm(COL), vm(2, COL), vm(3, 8),
            vm(8), vm(8), pltpu.VMEM((2, 8, tl, tl), F32),
            pltpu.SemaphoreType.DMA((56,)), pltpu.SemaphoreType.DMA((56,)), pltpu.SemaphoreType.DMA((5,)),
        ],
        compiler_params=pltpu.CompilerParams(
            collective_id=0, has_side_effects=True, vmem_limit_bytes=56 * 1024 * 1024),
    )(rows_one, parent_two, order_two, inverse_top, panel_one, base_one, panel_two, link_two, base_two)
    return pl.pallas_call(
        unpack, out_shape=(one, tile, one, tile, tile), in_specs=[vmem], out_specs=[vmem] * 5)(packed)


def solution(mesh):
    return jax.shard_map(
        local,
        mesh=mesh,
        in_specs=(
            P("prow", "pcol", None, None), P(), P("pcol", "prow", None, None), P("pcol", None, None), P(),
            P(), P("pcol", "prow", None, None), P("pcol", None, None), P("pcol", None, None),
        ),
        out_specs=(
            P("pcol", "prow", None, None), P("pcol", None, None), P("pcol", "prow", None, None),
            P("pcol", None, None), P("pcol", None, None),
        ),
        check_vma=False,
    )
```

```python
import functools

import jax
import jax.numpy as jnp
from jax import lax
from jax.experimental import pallas as pl
from jax.experimental.pallas import tpu as pltpu
from jax.sharding import PartitionSpec as P

F32 = jnp.float32
BF = jnp.bfloat16


def tdot(a, b):
    return lax.dot_general(a, b, (((0,), (0,)), ((), ())), preferred_element_type=F32)


def kernel(
    rows_ref, parent_ref, order_ref, inv_ref, p1_ref, b1_ref, p2_ref, link_ref, b2_ref,
    out_ref,
    tf, x1, x2, wb, yp, fb, nb, ys, yr, pz, lk, ub, uo, uu, ar, pv1, keep, snd, rcv, loc,
):
    tl = inv_ref.shape[-1]
    p = lax.axis_index("prow")
    c = lax.axis_index("pcol")
    x, yl = p // 2, p % 2
    yh, j, z, q = c // 8, c // 2, (c // 2) % 4, c % 2
    xl, xr, xo = (x + 3) % 4, (x + 1) % 4, (x + 2) % 4
    zl, zr, zo = (z + 3) % 4, (z + 1) % 4, (z + 2) % 4

    left_x = (2 * xl + yl, c)
    right_x = (2 * xr + yl, c)
    mate_y = (2 * x + 1 - yl, c)
    left_z = (p, 8 * yh + 2 * zl + q)
    right_z = (p, 8 * yh + 2 * zr + q)
    core = (p, 2 * j + 1 - q)
    far_y = (p, 8 * (1 - yh) + 2 * z + q)
    far_z = (p, 8 * yh + 2 * zo + q)

    def held(slot):
        return 4 * (slot % 2) + (slot // 2 + z) % 4

    to_p = 2 * ((z + 4 - p % 4) % 4) + yh
    turned = (to_p, 2 * p + q)
    source = (j, 2 * held(p) + q)
    stays = jnp.logical_and(to_p == p, c == 2 * p + q)

    parity = (yl, 1 - yl, 1 - yh, yh)
    level = (0, 0, 1, 1)

    def slot(t, xs):
        return 2 * xs + parity[t]

    def remote(src, dst, at, to, send_at=None):
        return pltpu.make_async_remote_copy(
            src_ref=src, dst_ref=dst, send_sem=snd.at[at if send_at is None else send_at], recv_sem=rcv.at[at],
            device_id=to, device_id_type=pl.DeviceIdType.MESH)

    T_AT, TURN_AT, MATE_AT, BASE_AT, FWD_AT, FWD_LEFT_AT = 0, 1, 3, 5, 13, 17
    FAR_AT, NE_AT, NL_AT, Y_AT, SWAP_AT, PZ_AT, LK_AT, UB_AT, UU_AT, A_AT = 21, 29, 37, 45, 47, 48, 52, 53, 56, 57
    panels = (p1_ref, p2_ref)
    slots_at = (x1.at[q], x2)

    def turn(l):
        return remote(panels[l].at[0], slots_at[l].at[to_p], TURN_AT + l, turned)

    def turn_here(l):
        return pltpu.make_async_copy(panels[l].at[0], slots_at[l].at[p], loc.at[l])

    def mate(l):
        return remote(slots_at[l].at[p], slots_at[l].at[p], MATE_AT + l, mate_y)

    def base(t, dr):
        at = slots_at[level[t]].at[slot(t, x)]
        return remote(at, at, BASE_AT + 2 * t + dr, (right_x, left_x)[dr])

    def base_in(t, dr):
        at = slots_at[level[t]].at[slot(t, (xl, xr)[dr])]
        return remote(at, at, BASE_AT + 2 * t + dr, right_x)

    def forward(t, dr):
        at = slots_at[level[t]].at[slot(t, (xl, xr)[dr]), pl.ds(4 * dr, 4)]
        return remote(at, at, FWD_AT + t, (right_x, left_x)[dr], (FWD_AT, FWD_LEFT_AT)[dr] + t)

    def forward_in(t):
        at = slots_at[level[t]].at[slot(t, xo)]
        return remote(at, at, FWD_AT + t, right_x)

    def far(t, dr):
        return remote(yp.at[t, zo, pl.ds(4 * dr, 4)], fb.at[t, dr], FAR_AT + 2 * t + dr, (right_z, left_z)[dr])

    def near_early(t, dr):
        part = pl.ds(4 - 4 * dr, 4)
        return remote(yp.at[t, (zr, zl)[dr], part], nb.at[t, dr, part], NE_AT + 2 * t + dr, (right_z, left_z)[dr])

    def near_late(t, dr):
        part = pl.ds(4 * dr, 4)
        return remote(yp.at[t, (zr, zl)[dr], part], nb.at[t, dr, part], NL_AT + 2 * t + dr, (right_z, left_z)[dr])

    def across(l):
        return remote(ys.at[l], yr.at[l], Y_AT + l, far_y)

    t_here = pltpu.make_async_copy(inv_ref, tf.at[q], loc.at[2])
    t_here.start()
    v1 = pltpu.make_async_copy(p1_ref.at[0], pv1, loc.at[3])
    v2 = pltpu.make_async_copy(p2_ref.at[0], pz.at[z, pl.ds(0, 8)], loc.at[4])
    v3 = pltpu.make_async_copy(link_ref.at[0], pz.at[z, 8], loc.at[5])
    v1.start()
    v2.start()
    v3.start()

    barrier = pltpu.get_barrier_semaphore()

    def greet(to):
        pl.semaphore_signal(barrier, inc=1, device_id=to, device_id_type=pl.DeviceIdType.MESH)

    @pl.when(jnp.logical_not(stays))
    def _():
        greet(source)

    for d in range(1, 8):
        greet(((p + d) % 8, c))
    for to in (left_z, right_z, core, far_y, far_z):
        greet(to)

    @pl.when(jnp.logical_not(stays))
    def _():
        pl.semaphore_wait(barrier, 13)

    @pl.when(stays)
    def _():
        pl.semaphore_wait(barrier, 12)

    def start_turn(l):
        @pl.when(jnp.logical_not(stays))
        def _():
            turn(l).start()

        @pl.when(stays)
        def _():
            turn_here(l).start()

    def wait_turn(l):
        @pl.when(jnp.logical_not(stays))
        def _():
            remote(slots_at[l].at[p], slots_at[l].at[p], TURN_AT + l, right_x).wait_recv()

        @pl.when(stays)
        def _():
            turn_here(l).wait()

    sent = []

    def go(copy):
        copy.start()
        sent.append(copy)

    def wait_mate(l):
        s = 2 * x + 1 - yl
        remote(slots_at[l].at[s], slots_at[l].at[s], MATE_AT + l, right_x).wait_recv()

    def base_out(t):
        go(base(t, 0))
        go(base(t, 1))

    def relay(t):
        for dr in range(2):
            base_in(t, dr).wait_recv()
            go(forward(t, dr))

    def row_at(l, k, i):
        if l == 0:
            return rows_ref[k, i]
        return rows_ref[parent_ref[k], order_ref[k, i]]

    def products(t, xs):
        l, s, zh = level[t], slot(t, xs), (xs + z) % 4
        k = 2 * held(s) + q
        cols = [row_at(l, k, 8 * j + n) for n in range(8)]
        cols = [((a >> 3) & 1, a & 7) for a in cols]
        if l == 1:
            par = parent_ref[k]
            at = 2 * (((par >> 1) + 4 - z) & 3) + ((par >> 3) & 1)
            above = jnp.concatenate([x1[par & 1, at, order_ref[k, 8 * j + n] & 7] for n in range(8)], axis=0)
            taken = jnp.dot(above, lk[s % 2, zh], preferred_element_type=F32)
            wb[...] = (x2[s].reshape(8 * tl, tl).astype(F32) - taken).astype(BF)

        def one(m, carry):
            r = row_at(l, k, 8 * p + m) & 15
            wide = jnp.concatenate([tf[a, r, b] for a, b in cols], axis=1)
            tall = wb[...] if l else x1[q, s].reshape(8 * tl, tl)
            yp[t, zh, m] = jnp.dot(wide, tall, preferred_element_type=F32).astype(BF)
            return carry

        lax.fori_loop(0, 8, one, 0)

        @pl.when(xs == 2)
        def _():
            far(t, 0).start()
            far(t, 1).start()

        @pl.when(xs == 1)
        def _():
            near_early(t, 0).start()

        @pl.when(xs == 3)
        def _():
            near_early(t, 1).start()

    def pass_on(t):
        for dr in range(2):
            far(t, dr).wait_recv()
            zh, part = (zr, zl)[dr], pl.ds(4 * dr, 4)
            yp[t, zh, part] = (yp[t, zh, part].astype(F32) + fb[t, dr].astype(F32)).astype(BF)
            go(near_late(t, dr))

    def meet(t):
        l = level[t]
        for dr in range(2):
            near_early(t, dr).wait_recv()
            near_late(t, dr).wait_recv()

        def total(m):
            return yp[t, z, m].astype(F32) + nb[t, 0, m].astype(F32) + nb[t, 1, m].astype(F32)

        def cross():
            for m in range(8):
                ys[l, m] = total(m).astype(BF)
            across(l).start()

        def stay():
            for m in range(8):
                keep[l, m] = total(m)

        if t == 2:
            cross()
        elif t == 3:
            stay()
        else:
            pl.when(parity[t] != yh)(cross)
            pl.when(parity[t] == yh)(stay)

    def spread(t):
        for d in range(1, 8):
            remote(ar.at[t, p], ar.at[t, p], A_AT + t, ((p + d) % 8, c)).start()

    def spread_all(t):
        return remote(ar.at[t, pl.ds(0, 7)], ar.at[t, pl.ds(0, 7)], A_AT + t, right_x)

    def spread_sum(t):
        spread_all(t).wait_recv()
        total = ar[t, 0].astype(F32)
        for i in range(1, 8):
            total = total + ar[t, i].astype(F32)
        return total

    def swap(s):
        remote(x1.at[q, s], x1.at[q, s], SWAP_AT, core).start()

    def swap_all():
        return remote(x1.at[1 - q], x1.at[1 - q], SWAP_AT, core)

    def child_in(dr):
        at = pz.at[(zl, zr)[dr]]
        return remote(at, at, PZ_AT + dr, right_z)

    def child_on(dr):
        at = pz.at[(zl, zr)[dr], pl.ds(5 * dr, 5 - dr)]
        return remote(at, at, PZ_AT + 2, (right_z, left_z)[dr], PZ_AT + 2 + dr)

    start_turn(0)
    t_there = remote(inv_ref, tf.at[q], T_AT, core)
    go(t_there)
    wait_turn(0)
    go(mate(0))
    base_out(0)
    start_turn(1)
    v2.wait()
    v3.wait()
    for dr in range(2):
        go(remote(pz.at[z], pz.at[z], PZ_AT + dr, (right_z, left_z)[dr]))
    swap(p)
    t_here.wait()
    t_there.wait_recv()
    products(0, x)
    wait_mate(0)
    base_out(1)
    swap(2 * x + 1 - yl)
    relay(0)
    swap(slot(0, xl))
    swap(slot(0, xr))
    for dr in range(2):
        child_in(dr).wait_recv()
        go(child_on(dr))
    products(1, x)
    products(0, xl)
    products(0, xr)
    wait_turn(1)
    go(mate(1))
    forward_in(0).wait_recv()
    swap(slot(0, xo))
    products(0, xo)
    wait_mate(1)
    base_out(2)
    relay(1)
    swap(slot(1, xl))
    swap(slot(1, xr))
    products(1, xl)
    products(1, xr)
    pass_on(0)
    base_out(3)
    remote(pz.at[zo], pz.at[zo], PZ_AT + 2, right_z).wait_recv()
    for i in range(4):
        lk[yh, i] = pz[i, 8]
    links = remote(lk.at[yh], lk.at[yh], LK_AT, far_y)
    go(links)
    forward_in(1).wait_recv()
    swap(slot(1, xo))
    products(1, xo)
    relay(2)
    meet(0)
    pass_on(1)
    swap_all().wait_recv()
    links.wait_recv()
    products(2, x)
    products(3, x)
    products(2, xl)
    products(2, xr)
    meet(1)
    relay(3)
    forward_in(2).wait_recv()
    products(2, xo)
    v1.wait()

    across(0).wait_recv()
    for m in range(8):
        tile = (-(keep[0, m] + yr[0, m].astype(F32))).astype(BF)
        out_ref[m] = tile
        ub[yh, q, m] = tile
    share = tdot(pv1[...].reshape(8 * tl, tl), ub[yh, q, pl.ds(0, 8)].reshape(8 * tl, tl))
    ar[0, p] = share.astype(BF)
    first = jnp.where(p == 0, 1.0, 0.0).astype(F32)
    ub[yh, q, 8] = (b1_ref[0] * first - share).astype(BF)
    go(remote(ub.at[yh, q], ub.at[yh, q], UB_AT, far_y))
    go(remote(ub.at[yh, q], ub.at[yh, q], UB_AT + 1, core))
    spread(0)

    pass_on(2)
    products(3, xl)
    products(3, xr)
    forward_in(3).wait_recv()
    products(3, xo)
    remote(ub.at[1 - yh, q], ub.at[1 - yh, q], UB_AT, far_y).wait_recv()
    go(remote(ub.at[1 - yh, q], ub.at[1 - yh, q], UB_AT + 2, core))
    meet(2)
    pass_on(3)

    out_ref[16] = (b1_ref[0] - spread_sum(0)).astype(BF)

    remote(ub.at[yh, 1 - q], ub.at[yh, 1 - q], UB_AT + 1, core).wait_recv()
    remote(ub.at[1 - yh, 1 - q], ub.at[1 - yh, 1 - q], UB_AT + 2, core).wait_recv()

    def child(d, carry):
        zc = (z + d) % 4
        k = 8 * yh + 2 * zc + q
        par = parent_ref[k]
        py, pq = (par >> 3) & 1, par & 1
        near = jnp.concatenate([ub[py, pq, order_ref[k, 8 * p + m] & 7] for m in range(8)], axis=0)
        total = tdot(near, pz[zc, pl.ds(0, 8)].reshape(8 * tl, tl))
        total = total + jnp.dot(ub[py, pq, 8], pz[zc, 8], preferred_element_type=F32)
        uo[d] = total.astype(BF)
        return carry

    lax.fori_loop(0, 4, child, 0)
    uu[z] = uo[0]
    for d, to in ((1, right_z), (2, far_z), (3, left_z)):
        remote(uo.at[d], uu.at[z], UU_AT, to).start()
    uu_all = remote(uu.at[pl.ds(0, 3)], uu.at[pl.ds(0, 3)], UU_AT, far_z)
    meet(3)
    uu_all.wait_recv()
    ar[1, p] = uu[(parent_ref[c] >> 1) & 3]
    spread(1)

    across(1).wait_recv()
    for m in range(8):
        out_ref[8 + m] = (-(keep[1, m] + yr[1, m].astype(F32))).astype(BF)
    lower = tdot(pz[z, pl.ds(0, 8)].reshape(8 * tl, tl), out_ref[pl.ds(8, 8)].reshape(8 * tl, tl))
    ar[2, p] = lower.astype(BF)
    spread(2)
    u2 = (-spread_sum(1)).astype(BF)
    out_ref[17] = u2
    rest = b2_ref[0] - tdot(pz[z, 8], u2)
    out_ref[18] = (rest - spread_sum(2)).astype(BF)
    swap_all().wait_send()
    uu_all.wait_send()

    for copy in sent:
        copy.wait_send()
    for l in range(2):
        @pl.when(jnp.logical_not(stays))
        def _():
            turn(l).wait_send()

        across(l).wait_send()
    for t in range(4):
        for dr in range(2):
            far(t, dr).wait_send()
            near_early(t, dr).wait_send()
    for t in range(3):
        spread_all(t).wait_send()


def unpack(all_ref, c1_ref, d1_ref, c2_ref, u2_ref, d2_ref):
    c1_ref[0] = all_ref[pl.ds(0, 8)]
    c2_ref[0] = all_ref[pl.ds(8, 8)]
    d1_ref[0] = all_ref[16]
    u2_ref[0] = all_ref[17]
    d2_ref[0] = all_ref[18]


def local(inverse_top, rows_one, panel_one, base_one, parent_two, order_two, panel_two, link_two, base_two):
    tl = inverse_top.shape[-1]
    vm = lambda *s: pltpu.VMEM(s + (tl, tl), BF)
    anyw = pl.BlockSpec(memory_space=pl.ANY)
    smem = pl.BlockSpec(memory_space=pltpu.SMEM)
    vmem = pl.BlockSpec(memory_space=pltpu.VMEM)
    one = jax.ShapeDtypeStruct(panel_one.shape, BF)
    tile = jax.ShapeDtypeStruct(link_two.shape, BF)
    packed = pl.pallas_call(
        kernel,
        out_shape=jax.ShapeDtypeStruct((19, tl, tl), BF),
        in_specs=[smem, smem, smem, anyw, anyw, vmem, anyw, anyw, vmem],
        out_specs=vmem,
        scratch_shapes=[
            vm(2, 16, 8), vm(2, 8, 8), vm(8, 8), pltpu.VMEM((8 * tl, tl), BF), vm(4, 4, 8),
            vm(4, 2, 4), vm(4, 2, 8), vm(2, 8), vm(2, 8),
            vm(4, 9), vm(2, 4), vm(2, 2, 9), vm(4), vm(4), vm(3, 8),
            vm(8), pltpu.VMEM((2, 8, tl, tl), F32),
            pltpu.SemaphoreType.DMA((60,)), pltpu.SemaphoreType.DMA((60,)), pltpu.SemaphoreType.DMA((6,)),
        ],
        compiler_params=pltpu.CompilerParams(
            collective_id=0, has_side_effects=True, vmem_limit_bytes=56 * 1024 * 1024),
    )(rows_one, parent_two, order_two, inverse_top, panel_one, base_one, panel_two, link_two, base_two)
    return pl.pallas_call(
        unpack, out_shape=(one, tile, one, tile, tile), in_specs=[vmem], out_specs=[vmem] * 5)(packed)


def solution(mesh):
    return jax.shard_map(
        local,
        mesh=mesh,
        in_specs=(
            P("prow", "pcol", None, None), P(), P("pcol", "prow", None, None), P("pcol", None, None), P(),
            P(), P("pcol", "prow", None, None), P("pcol", None, None), P("pcol", None, None),
        ),
        out_specs=(
            P("pcol", "prow", None, None), P("pcol", None, None), P("pcol", "prow", None, None),
            P("pcol", None, None), P("pcol", None, None),
        ),
        check_vma=False,
    )
```

```python
import functools

import jax
import jax.numpy as jnp
from jax import lax
from jax.experimental import pallas as pl
from jax.experimental.pallas import tpu as pltpu
from jax.sharding import PartitionSpec as P

F32 = jnp.float32
BF = jnp.bfloat16


def tdot(a, b):
    return lax.dot_general(a, b, (((0,), (0,)), ((), ())), preferred_element_type=F32)


def kernel(
    rows_ref, parent_ref, order_ref, inv_ref, p1_ref, b1_ref, p2_ref, link_ref, b2_ref,
    out_ref,
    tf, x1, x2, wb, yp, fb, nb, ys, yr, pz, lk, ub, uo, uu, ar, pr, fn, pv1, keep, snd, rcv, loc,
):
    tl = inv_ref.shape[-1]
    p = lax.axis_index("prow")
    c = lax.axis_index("pcol")
    x, yl = p // 2, p % 2
    yh, j, z, q = c // 8, c // 2, (c // 2) % 4, c % 2
    xl, xr, xo = (x + 3) % 4, (x + 1) % 4, (x + 2) % 4
    zl, zr, zo = (z + 3) % 4, (z + 1) % 4, (z + 2) % 4

    left_x = (2 * xl + yl, c)
    right_x = (2 * xr + yl, c)
    mate_y = (2 * x + 1 - yl, c)
    left_z = (p, 8 * yh + 2 * zl + q)
    right_z = (p, 8 * yh + 2 * zr + q)
    core = (p, 2 * j + 1 - q)
    far_y = (p, 8 * (1 - yh) + 2 * z + q)
    far_z = (p, 8 * yh + 2 * zo + q)

    def held(slot):
        return 4 * (slot % 2) + (slot // 2 + z) % 4

    to_p = 2 * ((z + 4 - p % 4) % 4) + yh
    turned = (to_p, 2 * p + q)
    source = (j, 2 * held(p) + q)
    stays = jnp.logical_and(to_p == p, c == 2 * p + q)

    parity = (yl, 1 - yl, 1 - yh, yh)
    level = (0, 0, 1, 1)

    def slot(t, xs):
        return 2 * xs + parity[t]

    def remote(src, dst, at, to, send_at=None):
        return pltpu.make_async_remote_copy(
            src_ref=src, dst_ref=dst, send_sem=snd.at[at if send_at is None else send_at], recv_sem=rcv.at[at],
            device_id=to, device_id_type=pl.DeviceIdType.MESH)

    T_AT, TURN_AT, MATE_AT, BASE_AT, FWD_AT, FWD_LEFT_AT = 0, 1, 3, 5, 13, 17
    FAR_AT, NE_AT, NL_AT, Y_AT, SWAP_AT, PZ_AT, LK_AT, UB_AT, UU_AT, A_AT, B_AT = 21, 29, 37, 45, 47, 48, 52, 53, 56, 57, 60
    panels = (p1_ref, p2_ref)
    slots_at = (x1.at[q], x2)

    def turn(l):
        return remote(panels[l].at[0], slots_at[l].at[to_p], TURN_AT + l, turned)

    def turn_here(l):
        return pltpu.make_async_copy(panels[l].at[0], slots_at[l].at[p], loc.at[l])

    def mate(l):
        return remote(slots_at[l].at[p], slots_at[l].at[p], MATE_AT + l, mate_y)

    def base(t, dr):
        at = slots_at[level[t]].at[slot(t, x)]
        return remote(at, at, BASE_AT + 2 * t + dr, (right_x, left_x)[dr])

    def base_in(t, dr):
        at = slots_at[level[t]].at[slot(t, (xl, xr)[dr])]
        return remote(at, at, BASE_AT + 2 * t + dr, right_x)

    def forward(t, dr):
        at = slots_at[level[t]].at[slot(t, (xl, xr)[dr]), pl.ds(4 * dr, 4)]
        return remote(at, at, FWD_AT + t, (right_x, left_x)[dr], (FWD_AT, FWD_LEFT_AT)[dr] + t)

    def forward_in(t):
        at = slots_at[level[t]].at[slot(t, xo)]
        return remote(at, at, FWD_AT + t, right_x)

    def far(t, dr):
        return remote(yp.at[t, zo, pl.ds(4 * dr, 4)], fb.at[t, dr], FAR_AT + 2 * t + dr, (right_z, left_z)[dr])

    def near_early(t, dr):
        part = pl.ds(4 - 4 * dr, 4)
        return remote(yp.at[t, (zr, zl)[dr], part], nb.at[t, dr, part], NE_AT + 2 * t + dr, (right_z, left_z)[dr])

    def near_late(t, dr):
        part = pl.ds(4 * dr, 4)
        return remote(yp.at[t, (zr, zl)[dr], part], nb.at[t, dr, part], NL_AT + 2 * t + dr, (right_z, left_z)[dr])

    def across(l):
        return remote(ys.at[l], yr.at[l], Y_AT + l, far_y)

    t_here = pltpu.make_async_copy(inv_ref, tf.at[q], loc.at[2])
    t_here.start()
    v1 = pltpu.make_async_copy(p1_ref.at[0], pv1, loc.at[3])
    v2 = pltpu.make_async_copy(p2_ref.at[0], pz.at[z, pl.ds(0, 8)], loc.at[4])
    v3 = pltpu.make_async_copy(link_ref.at[0], pz.at[z, 8], loc.at[5])
    v1.start()
    v2.start()
    v3.start()

    barrier = pltpu.get_barrier_semaphore()

    def greet(to):
        pl.semaphore_signal(barrier, inc=1, device_id=to, device_id_type=pl.DeviceIdType.MESH)

    @pl.when(jnp.logical_not(stays))
    def _():
        greet(source)

    for d in range(1, 8):
        greet(((p + d) % 8, c))
    for to in (left_z, right_z, core, far_y, far_z):
        greet(to)

    @pl.when(jnp.logical_not(stays))
    def _():
        pl.semaphore_wait(barrier, 13)

    @pl.when(stays)
    def _():
        pl.semaphore_wait(barrier, 12)

    def start_turn(l):
        @pl.when(jnp.logical_not(stays))
        def _():
            turn(l).start()

        @pl.when(stays)
        def _():
            turn_here(l).start()

    def wait_turn(l):
        @pl.when(jnp.logical_not(stays))
        def _():
            remote(slots_at[l].at[p], slots_at[l].at[p], TURN_AT + l, right_x).wait_recv()

        @pl.when(stays)
        def _():
            turn_here(l).wait()

    sent = []

    def go(copy):
        copy.start()
        sent.append(copy)

    def wait_mate(l):
        s = 2 * x + 1 - yl
        remote(slots_at[l].at[s], slots_at[l].at[s], MATE_AT + l, right_x).wait_recv()

    def base_out(t):
        go(base(t, 0))
        go(base(t, 1))

    own_last = yl == yh

    def both(t):
        for dr in range(2):
            base(t, dr).start()

    def own_out():
        pl.when(own_last)(lambda: both(3))
        pl.when(jnp.logical_not(own_last))(lambda: both(2))

    def mate_out():
        pl.when(own_last)(lambda: both(2))
        pl.when(jnp.logical_not(own_last))(lambda: both(3))

    def relay(t):
        for dr in range(2):
            base_in(t, dr).wait_recv()
            go(forward(t, dr))

    def row_at(l, k, i):
        if l == 0:
            return rows_ref[k, i]
        return rows_ref[parent_ref[k], order_ref[k, i]]

    def products(t, xs):
        l, s, zh = level[t], slot(t, xs), (xs + z) % 4
        k = 2 * held(s) + q
        cols = [row_at(l, k, 8 * j + n) for n in range(8)]
        cols = [((a >> 3) & 1, a & 7) for a in cols]
        if l == 1:
            par = parent_ref[k]
            at = 2 * (((par >> 1) + 4 - z) & 3) + ((par >> 3) & 1)
            above = jnp.concatenate([x1[par & 1, at, order_ref[k, 8 * j + n] & 7] for n in range(8)], axis=0)
            taken = jnp.dot(above, lk[s % 2, zh], preferred_element_type=F32)
            wb[...] = (x2[s].reshape(8 * tl, tl).astype(F32) - taken).astype(BF)

        def some(i, carry):
            wides = []
            for m in range(4):
                r = row_at(l, k, 8 * p + 4 * i + m) & 15
                wides.append(jnp.concatenate([tf[a, r, b] for a, b in cols], axis=1))
            wide = jnp.concatenate(wides, axis=0)
            tall = wb[...] if l else x1[q, s].reshape(8 * tl, tl)
            yp[t, zh, pl.ds(4 * i, 4)] = jnp.dot(
                wide, tall, preferred_element_type=F32).astype(BF).reshape(4, tl, tl)
            return carry

        lax.fori_loop(0, 8 // 4, some, 0)

        @pl.when(xs == 2)
        def _():
            far(t, 0).start()
            far(t, 1).start()

        @pl.when(xs == 1)
        def _():
            near_early(t, 0).start()

        @pl.when(xs == 3)
        def _():
            near_early(t, 1).start()

    def pass_on(t):
        for dr in range(2):
            far(t, dr).wait_recv()
            zh, part = (zr, zl)[dr], pl.ds(4 * dr, 4)
            yp[t, zh, part] = (yp[t, zh, part].astype(F32) + fb[t, dr].astype(F32)).astype(BF)
            go(near_late(t, dr))

    def meet(t):
        l = level[t]
        for dr in range(2):
            near_early(t, dr).wait_recv()
            near_late(t, dr).wait_recv()

        def total(m):
            return yp[t, z, m].astype(F32) + nb[t, 0, m].astype(F32) + nb[t, 1, m].astype(F32)

        def cross():
            for m in range(8):
                ys[l, m] = total(m).astype(BF)
            across(l).start()

        def stay():
            for m in range(8):
                keep[l, m] = total(m)

        if t == 2:
            cross()
        elif t == 3:
            stay()
        else:
            pl.when(parity[t] != yh)(cross)
            pl.when(parity[t] == yh)(stay)

    rp = tl // 8

    def rows_of(i):
        return pl.ds(pl.multiple_of(i * rp, rp), rp)

    def spread(t, value):
        ar[t] = value
        pr[t, p] = ar[t, rows_of(p)]
        for d in range(1, 8):
            i = (p + d) % 8
            remote(ar.at[t, rows_of(i)], pr.at[t, p], A_AT + t, (i, c)).start()

    def spread_all(t):
        return remote(pr.at[t, pl.ds(0, 7)], pr.at[t, pl.ds(0, 7)], A_AT + t, right_x)

    def spread_sum(t):
        spread_all(t).wait_recv()
        total = pr[t, 0].astype(F32)
        for i in range(1, 8):
            total = total + pr[t, i].astype(F32)
        return total

    def hand_out(t, value):
        fn[t, rows_of(p)] = value.astype(BF)
        for d in range(1, 8):
            at = fn.at[t, rows_of(p)]
            remote(at, at, B_AT + t, ((p + d) % 8, c)).start()

    def hand_all(t):
        at = fn.at[t, pl.ds(0, 7 * rp)]
        return remote(at, at, B_AT + t, right_x)

    def swap(s):
        remote(x1.at[q, s], x1.at[q, s], SWAP_AT, core).start()

    def swap_all():
        return remote(x1.at[1 - q], x1.at[1 - q], SWAP_AT, core)

    def child_in(dr):
        at = pz.at[(zl, zr)[dr]]
        return remote(at, at, PZ_AT + dr, right_z)

    def child_on(dr):
        at = pz.at[(zl, zr)[dr], pl.ds(5 * dr, 5 - dr)]
        return remote(at, at, PZ_AT + 2, (right_z, left_z)[dr], PZ_AT + 2 + dr)

    start_turn(0)
    start_turn(1)
    t_there = remote(inv_ref, tf.at[q], T_AT, core)
    go(t_there)
    wait_turn(0)
    go(mate(0))
    base_out(0)
    v2.wait()
    v3.wait()
    for dr in range(2):
        go(remote(pz.at[z], pz.at[z], PZ_AT + dr, (right_z, left_z)[dr]))
    swap(p)
    t_here.wait()
    t_there.wait_recv()
    products(0, x)
    wait_mate(0)
    base_out(1)
    swap(2 * x + 1 - yl)
    relay(0)
    swap(slot(0, xl))
    swap(slot(0, xr))
    for dr in range(2):
        child_in(dr).wait_recv()
        go(child_on(dr))
    products(1, x)
    products(0, xl)
    products(0, xr)
    wait_turn(1)
    go(mate(1))
    own_out()
    forward_in(0).wait_recv()
    swap(slot(0, xo))
    products(0, xo)
    relay(1)
    wait_mate(1)
    mate_out()
    swap(slot(1, xl))
    swap(slot(1, xr))
    products(1, xl)
    products(1, xr)
    pass_on(0)
    remote(pz.at[zo], pz.at[zo], PZ_AT + 2, right_z).wait_recv()
    for i in range(4):
        lk[yh, i] = pz[i, 8]
    links = remote(lk.at[yh], lk.at[yh], LK_AT, far_y)
    go(links)
    forward_in(1).wait_recv()
    swap(slot(1, xo))
    products(1, xo)
    relay(2)
    meet(0)
    pass_on(1)
    swap_all().wait_recv()
    links.wait_recv()
    products(2, x)
    products(3, x)
    products(2, xl)
    products(2, xr)
    meet(1)
    relay(3)
    forward_in(2).wait_recv()
    products(2, xo)
    v1.wait()

    across(0).wait_recv()
    for m in range(8):
        tile = (-(keep[0, m] + yr[0, m].astype(F32))).astype(BF)
        out_ref[m] = tile
        ub[yh, q, m] = tile
    share = tdot(pv1[...].reshape(8 * tl, tl), ub[yh, q, pl.ds(0, 8)].reshape(8 * tl, tl))
    first = jnp.where(p == 0, 1.0, 0.0).astype(F32)
    ub[yh, q, 8] = (b1_ref[0] * first - share).astype(BF)
    go(remote(ub.at[yh, q], ub.at[yh, q], UB_AT, far_y))
    go(remote(ub.at[yh, q], ub.at[yh, q], UB_AT + 1, core))
    spread(0, share.astype(BF))

    pass_on(2)
    products(3, xl)
    products(3, xr)
    forward_in(3).wait_recv()
    products(3, xo)
    remote(ub.at[1 - yh, q], ub.at[1 - yh, q], UB_AT, far_y).wait_recv()
    go(remote(ub.at[1 - yh, q], ub.at[1 - yh, q], UB_AT + 2, core))
    meet(2)
    pass_on(3)

    hand_out(0, b1_ref[0, rows_of(p)] - spread_sum(0))

    remote(ub.at[yh, 1 - q], ub.at[yh, 1 - q], UB_AT + 1, core).wait_recv()
    remote(ub.at[1 - yh, 1 - q], ub.at[1 - yh, 1 - q], UB_AT + 2, core).wait_recv()

    def child(d, carry):
        zc = (z + d) % 4
        k = 8 * yh + 2 * zc + q
        par = parent_ref[k]
        py, pq = (par >> 3) & 1, par & 1
        near = jnp.concatenate([ub[py, pq, order_ref[k, 8 * p + m] & 7] for m in range(8)], axis=0)
        total = tdot(near, pz[zc, pl.ds(0, 8)].reshape(8 * tl, tl))
        total = total + jnp.dot(ub[py, pq, 8], pz[zc, 8], preferred_element_type=F32)
        uo[d] = total.astype(BF)
        return carry

    lax.fori_loop(0, 4, child, 0)
    uu[z] = uo[0]
    for d, to in ((1, right_z), (2, far_z), (3, left_z)):
        remote(uo.at[d], uu.at[z], UU_AT, to).start()
    uu_all = remote(uu.at[pl.ds(0, 3)], uu.at[pl.ds(0, 3)], UU_AT, far_z)
    meet(3)
    uu_all.wait_recv()
    upper = uu[(parent_ref[c] >> 1) & 3]
    spread(1, upper)
    linked = tdot(pz[z, 8], upper)

    across(1).wait_recv()
    for m in range(8):
        out_ref[8 + m] = (-(keep[1, m] + yr[1, m].astype(F32))).astype(BF)
    lower = tdot(pz[z, pl.ds(0, 8)].reshape(8 * tl, tl), out_ref[pl.ds(8, 8)].reshape(8 * tl, tl))
    spread(2, (lower - linked).astype(BF))
    hand_out(1, -spread_sum(1))
    hand_out(2, b2_ref[0, rows_of(p)] - spread_sum(2))
    for t in range(3):
        hand_all(t).wait_recv()
        out_ref[16 + t] = fn[t]
    swap_all().wait_send()
    uu_all.wait_send()

    for t in (2, 3):
        for dr in range(2):
            base(t, dr).wait_send()
    for copy in sent:
        copy.wait_send()
    for l in range(2):
        @pl.when(jnp.logical_not(stays))
        def _():
            turn(l).wait_send()

        across(l).wait_send()
    for t in range(4):
        for dr in range(2):
            far(t, dr).wait_send()
            near_early(t, dr).wait_send()
    for t in range(3):
        spread_all(t).wait_send()
        hand_all(t).wait_send()


def unpack(all_ref, c1_ref, d1_ref, c2_ref, u2_ref, d2_ref):
    c1_ref[0] = all_ref[pl.ds(0, 8)]
    c2_ref[0] = all_ref[pl.ds(8, 8)]
    d1_ref[0] = all_ref[16]
    u2_ref[0] = all_ref[17]
    d2_ref[0] = all_ref[18]


def local(inverse_top, rows_one, panel_one, base_one, parent_two, order_two, panel_two, link_two, base_two):
    tl = inverse_top.shape[-1]
    vm = lambda *s: pltpu.VMEM(s + (tl, tl), BF)
    anyw = pl.BlockSpec(memory_space=pl.ANY)
    smem = pl.BlockSpec(memory_space=pltpu.SMEM)
    vmem = pl.BlockSpec(memory_space=pltpu.VMEM)
    one = jax.ShapeDtypeStruct(panel_one.shape, BF)
    tile = jax.ShapeDtypeStruct(link_two.shape, BF)
    packed = pl.pallas_call(
        kernel,
        out_shape=jax.ShapeDtypeStruct((19, tl, tl), BF),
        in_specs=[smem, smem, smem, anyw, anyw, vmem, anyw, anyw, vmem],
        out_specs=vmem,
        scratch_shapes=[
            vm(2, 16, 8), vm(2, 8, 8), vm(8, 8), pltpu.VMEM((8 * tl, tl), BF), vm(4, 4, 8),
            vm(4, 2, 4), vm(4, 2, 8), vm(2, 8), vm(2, 8),
            vm(4, 9), vm(2, 4), vm(2, 2, 9), vm(4), vm(4), vm(3), pltpu.VMEM((3, 8, tl // 8, tl), BF), vm(3),
            vm(8), pltpu.VMEM((2, 8, tl, tl), F32),
            pltpu.SemaphoreType.DMA((63,)), pltpu.SemaphoreType.DMA((63,)), pltpu.SemaphoreType.DMA((6,)),
        ],
        compiler_params=pltpu.CompilerParams(
            collective_id=0, has_side_effects=True, vmem_limit_bytes=56 * 1024 * 1024),
    )(rows_one, parent_two, order_two, inverse_top, panel_one, base_one, panel_two, link_two, base_two)
    return pl.pallas_call(
        unpack, out_shape=(one, tile, one, tile, tile), in_specs=[vmem], out_specs=[vmem] * 5)(packed)


def solution(mesh):
    return jax.shard_map(
        local,
        mesh=mesh,
        in_specs=(
            P("prow", "pcol", None, None), P(), P("pcol", "prow", None, None), P("pcol", None, None), P(),
            P(), P("pcol", "prow", None, None), P("pcol", None, None), P("pcol", None, None),
        ),
        out_specs=(
            P("pcol", "prow", None, None), P("pcol", None, None), P("pcol", "prow", None, None),
            P("pcol", None, None), P("pcol", None, None),
        ),
        check_vma=False,
    )
```
